32 devices in a mesh: seq: 16 (over z, y, x), head: 2 (over core).
Axes of the slice: x: 2, y: 2, z: 4, core: 2. Of those that a mesh axis runs over, the one named last changes fastest.
Arguments:
- query_in: bfloat16 [8192, 4096], P('seq', 'head'), may hold values from -128 to 128
- key_in: bfloat16 [8192, 4096], P('seq', 'head'), may hold values from -6 to 6
- value_in: bfloat16 [8192, 4096], P('seq', 'head'), may hold values from -6 to 6
- upstream: bfloat16 [8192, 4096], P('seq', 'head'), may hold values from -24 to 24
- norm_gain: float32 [4096], P('head'), may hold values from 0.1 to 1.9
- state_in: float32 [32, 128, 128], P('head'), may hold values from -96 to 96
Outputs:
- normed_out: bfloat16 [8192, 4096], P('seq', 'head')
- query_grad: bfloat16 [8192, 4096], P('seq', 'head')
- key_grad: bfloat16 [8192, 4096], P('seq', 'head')
- value_grad: bfloat16 [8192, 4096], P('seq', 'head')
- gain_grad: float32 [4096], P('head')
- state_grad: float32 [32, 128, 128], P('head')
The draws below stay inside these ranges and needn't reach their ends.
All inputs are finite; a program needn't handle non-finite values.
Results may differ from the reference program's by a relative error of at most 0.0026.
Values sent between devices are 32-bit elements; how exact they have to be, the bound alone decides.
No kernel may reach another device: no remote copies, remote signals or barrier semaphores. Data moves between devices by JAX's collectives and lax.ppermute only.
A program may use at most 128 MiB of HBM per device.

```python
import math
import jax
import jax.numpy as jnp
from jax import lax

HEADS = 32
HEAD = 128
TOK_DEV = 512
WIDTH = 4096
TOKENS = 8192
N_SEQ = 16


def draw_query_in(key, part):
    first, second = jax.random.split(key, 2)
    base = jnp.clip(jax.random.normal(first, (TOKENS, HEADS * HEAD), jnp.float32), -4.0, 4.0)
    rows = jnp.exp(jax.random.uniform(second, (TOKENS, 1), jnp.float32, 0.0, math.log(10.0)))
    head_index = (jnp.arange(HEADS * HEAD) // HEAD).astype(jnp.float32)
    columns = jnp.exp(0.5 * math.log(10.0) * head_index / max(HEADS - 1, 1))
    return (base * rows * columns[None, :]).astype(jnp.bfloat16)


def draw_upstream(key, part):
    first, second = jax.random.split(key, 2)
    base = jnp.clip(jax.random.normal(first, (TOKENS, HEADS * HEAD), jnp.float32), -4.0, 4.0)
    position = jnp.arange(TOKENS).astype(jnp.float32) / max(TOKENS - 1, 1)
    rising = jnp.exp(math.log(3.0) * position)[:, None]
    rows = jnp.exp(jax.random.uniform(second, (TOKENS, 1), jnp.float32, 0.0, math.log(2.0)))
    return (base * rising * rows).astype(jnp.bfloat16)


def levels(key, extent, cuts, smallest, largest):
    factor_of = 1.0
    for dim, parts in cuts:
        draws = jax.random.uniform(jax.random.fold_in(jax.random.fold_in(key, 6), dim), (parts,), jnp.float32, smallest / len(cuts), largest / len(cuts))
        factor_of = factor_of * jnp.repeat(jnp.exp(draws), extent[dim] // parts).reshape((-1,) + (1,) * (len(extent) - 1 - dim))
    return factor_of


def normal_values(own_key, extent, spread, bound, cuts=(), kind=jnp.bfloat16):
    level = levels(own_key, extent, cuts, -0.22, 0.18) if cuts else 1.0
    entries = jax.random.normal(own_key, extent, jnp.float32) * spread * level
    return jnp.minimum(jnp.maximum(entries, -bound), bound).astype(kind)


def setup_inputs(seed: int = 0) -> dict:
    key_of = jax.random.split(jax.random.key(seed), 7)
    query_in = draw_query_in(jax.random.fold_in(key_of[6], 71), 0)
    key_in = normal_values(key_of[1], (TOKENS, WIDTH), 1.0, 6.0, ((0, 16), (1, 2)))
    value_in = normal_values(key_of[2], (TOKENS, WIDTH), 1.0, 6.0, ((0, 16), (1, 2)))
    upstream = draw_upstream(jax.random.fold_in(key_of[6], 71), 0)
    norm_gain = jnp.clip(1.0 + 0.18 * jax.random.normal(key_of[4], (WIDTH,), jnp.float32), 0.1, 1.9)
    state_in = normal_values(key_of[5], (HEADS, HEAD, HEAD), 16.0, 96.0, ((0, 2),), jnp.float32)
    return dict(query_in=query_in, key_in=key_in, value_in=value_in, upstream=upstream, norm_gain=norm_gain, state_in=state_in)


def reference(query_in, key_in, value_in, upstream, norm_gain, state_in):
    block_shape = (N_SEQ, TOK_DEV, HEADS, HEAD)
    queries = query_in.reshape(block_shape)
    keys_all = key_in.reshape(block_shape)
    values_all = value_in.reshape(block_shape)
    causal = jnp.tril(jnp.ones((TOK_DEV, TOK_DEV), dtype=bool))[None]
    highest = lax.Precision.HIGHEST

    def block_scores(query_rows, key_rows):
        raw = jnp.einsum('thd,shd->hts', query_rows.astype(jnp.float32), key_rows.astype(jnp.float32))
        return jnp.where(causal, raw, 0.0).astype(jnp.bfloat16)

    def forward_step(running, pieces):
        query_rows, key_rows, value_rows = pieces
        scores = block_scores(query_rows, key_rows)
        inside = jnp.einsum('hts,she->the', scores.astype(jnp.float32), value_rows.astype(jnp.float32))
        carried = jnp.einsum('thd,hde->the', query_rows.astype(jnp.float32), running, precision=highest)
        grown = running + jnp.einsum('thd,the->hde', key_rows.astype(jnp.float32), value_rows.astype(jnp.float32))
        return (grown, (inside + carried, running))
    final_state, (attended, befores) = lax.scan(forward_step, state_in, (queries, keys_all, values_all))
    flattened = attended.reshape(TOKENS, WIDTH)
    mean_square = lax.optimization_barrier(jnp.mean(flattened * flattened, axis=1, keepdims=True))
    inverse = lax.rsqrt(mean_square + 1e-06)
    normed = flattened * inverse
    normed_out = (normed * norm_gain).astype(jnp.bfloat16)
    upstream_full = upstream.astype(jnp.float32)
    scaled = upstream_full * norm_gain
    product = lax.optimization_barrier(jnp.mean(scaled * flattened, axis=1, keepdims=True))
    d_full = inverse * (scaled - flattened * (product * inverse * inverse))
    gain_grad = lax.optimization_barrier(jnp.sum(upstream_full * normed, axis=0))
    d_low = d_full.astype(jnp.bfloat16)

    def backward_step(suffix, pieces):
        query_rows, key_rows, value_rows, full_rows, low_rows, running = pieces
        scores = block_scores(query_rows, key_rows)
        d_raw = jnp.einsum('the,she->hts', low_rows.astype(jnp.float32), value_rows.astype(jnp.float32))
        d_scores = jnp.where(causal, d_raw, 0.0).astype(jnp.bfloat16)
        query_part = jnp.einsum('hts,shd->thd', d_scores.astype(jnp.float32), key_rows.astype(jnp.float32))
        query_part = query_part + jnp.einsum('the,hde->thd', full_rows, running, precision=highest)
        key_part = jnp.einsum('hts,thd->shd', d_scores.astype(jnp.float32), query_rows.astype(jnp.float32))
        key_part = key_part + jnp.einsum('she,hde->shd', value_rows.astype(jnp.float32), suffix, precision=highest)
        value_part = jnp.einsum('hts,the->she', scores.astype(jnp.float32), low_rows.astype(jnp.float32))
        value_part = value_part + jnp.einsum('shd,hde->she', key_rows.astype(jnp.float32), suffix, precision=highest)
        grown = suffix + jnp.einsum('thd,the->hde', query_rows.astype(jnp.float32), low_rows.astype(jnp.float32))
        return (grown, (query_part.astype(jnp.bfloat16), key_part.astype(jnp.bfloat16), value_part.astype(jnp.bfloat16)))
    inputs_back = (queries, keys_all, values_all, d_full.reshape(block_shape), d_low.reshape(block_shape), befores)
    start_grad = jnp.zeros((HEADS, HEAD, HEAD), jnp.float32)
    state_grad, (query_grad, key_grad, value_grad) = lax.scan(backward_step, start_grad, inputs_back, reverse=True)
    return (normed_out, query_grad.reshape(TOKENS, WIDTH), key_grad.reshape(TOKENS, WIDTH), value_grad.reshape(TOKENS, WIDTH), gain_grad, state_grad)
```

```python
import functools

import jax
import jax.numpy as jnp
from jax import lax
from jax.experimental import pallas as pl
from jax.experimental.pallas import tpu as pltpu
from jax.sharding import PartitionSpec as P


PLANE = 4
F32, BF16 = jnp.float32, jnp.bfloat16


def mm(a, b, da, db):
    return lax.dot_general(a, b, (((da,), (db,)), ((), ())), preferred_element_type=F32)


def split2(x):
    hi = x.astype(BF16)
    return hi, (x - hi.astype(F32)).astype(BF16)


def split_cat(x, axis):
    return jnp.concatenate(split2(x), axis=axis)


def lower(x):
    r = lax.broadcasted_iota(jnp.int32, x.shape, 0)
    c = lax.broadcasted_iota(jnp.int32, x.shape, 1)
    return jnp.where(c <= r, x, 0.0).astype(BF16)


def upper(x):
    r = lax.broadcasted_iota(jnp.int32, x.shape, 0)
    c = lax.broadcasted_iota(jnp.int32, x.shape, 1)
    return jnp.where(r <= c, x, 0.0).astype(BF16)


def lower_rows(a, b):
    rows = a.shape[0]
    half = min(rows, 256)
    out = []
    for i in range(0, rows, half):
        diag = lower(mm(a[i : i + half], b[i : i + half], 1, 1))
        if i:
            left = mm(a[i : i + half], b[:i], 1, 1).astype(BF16)
            diag = jnp.concatenate([left, diag], axis=1)
        out.append(diag)
    return out, half


def upper_rows(a, b):
    rows = a.shape[0]
    half = min(rows, 256)
    out = []
    for i in range(0, rows, half):
        diag = upper(mm(a[i : i + half], b[i : i + half], 1, 1))
        if i + half < rows:
            right = mm(a[i : i + half], b[i + half :], 1, 1).astype(BF16)
            diag = jnp.concatenate([diag, right], axis=1)
        out.append(diag)
    return out, half


def lower_times(blocks, half, x):
    parts = [mm(s, x[: (i + 1) * half], 1, 0) for i, s in enumerate(blocks)]
    return jnp.concatenate(parts, axis=0)


def upper_times(blocks, half, x):
    parts = [mm(s, x[i * half :], 1, 0) for i, s in enumerate(blocks)]
    return jnp.concatenate(parts, axis=0)


def as_column(row):
    return jnp.broadcast_to(row, (128, row.shape[1])).T


def local_kernel(c_ref, k_ref, v_ref, *outs, hg):
    j = pl.program_id(0)
    size = k_ref.shape[1]
    product = mm(k_ref[...], v_ref[...], 0, 0)
    for g, out in enumerate(outs):
        @pl.when(j // hg == g)
        def _():
            out[pl.ds(pl.multiple_of((j % hg) * size, size), size), :] = product


def inside_kernel(c_ref, q_ref, k_ref, v_ref, o_ref):
    blocks, half = lower_rows(q_ref[...], k_ref[...])
    o_ref[...] = lower_times(blocks, half, v_ref[...])


def carried_kernel(c_ref, x_ref, q_ref, u_ref, g_ref, st_ref, sb_ref, *refs, hg, first, last):
    ins, outs = (refs[:0], refs) if first else (refs[:2], refs[2:])
    a_ref, s_ref, stat_ref = outs[:3]
    h = pl.program_id(0)
    state = st_ref[0] + sb_ref[...]
    s_ref[...] = state
    q = q_ref[...]
    a = x_ref[...] + mm(jnp.concatenate([q, q], axis=1), split_cat(state, 0), 1, 0)
    a_ref[...] = a

    @pl.when(h == 0)
    def _():
        stat_ref[...] = jnp.zeros_like(stat_ref) if first else ins[1][...]

    stat_ref[0] += a * a
    stat_ref[1] += (u_ref[...].astype(F32) * g_ref[...]) * a
    if last:
        @pl.when(h == hg - 1)
        def _():
            for i in range(2):
                outs[3][i : i + 1, :] = jnp.sum(stat_ref[i].T, axis=0, keepdims=True)


def row_terms(stat_ref, columns):
    inverse = lax.rsqrt(as_column(stat_ref[0:1, :]) / columns + 1e-06)
    return inverse, (as_column(stat_ref[1:2, :]) / columns) * inverse * inverse


def inner_kernel(c_ref, a_ref, q_ref, u_ref, g_ref, stat_ref, *outs, hg, columns):
    outs, (inv_ref, coef_ref) = outs[:-2], outs[-2:]
    j = pl.program_id(0)

    @pl.when(j == 0)
    def _():
        inv_ref[...], coef_ref[...] = row_terms(stat_ref, columns)
        for out in outs:
            out[hg * 128 :, :] = jnp.zeros_like(out[hg * 128 :, :])

    a, u, inverse = a_ref[...], u_ref[...].astype(F32), inv_ref[...]
    d = inverse * (u * g_ref[...] - a * coef_ref[...])
    product = mm(q_ref[...], d.astype(BF16), 0, 0)
    gain = jnp.sum(u * (a * inverse), axis=0, keepdims=True)
    size = product.shape[0]
    for g in range(len(outs)):
        @pl.when(j // hg == g)
        def _():
            h = j % hg
            outs[g][pl.ds(pl.multiple_of(h * size, size), size), :] = product
            for i in range(hg):
                @pl.when(h == i)
                def _():
                    outs[g][hg * size + i : hg * size + i + 1, :] = gain


def window_kernel(c_ref, a_ref, q_ref, k_ref, v_ref, u_ref, g_ref, stat_ref, s_ref, *refs, columns, first):
    n_ref, qg_ref, kp_ref, vp_ref, inv_ref, coef_ref = refs if first else refs[2:]

    @pl.when(pl.program_id(0) == 0)
    def _():
        inv_ref[...], coef_ref[...] = row_terms(stat_ref, columns)

    a, u, inverse, gain = a_ref[...], u_ref[...].astype(F32), inv_ref[...], g_ref[...]
    n_ref[...] = ((a * inverse) * gain).astype(BF16)
    d = inverse * (u * gain - a * coef_ref[...])
    dh, dl = split2(d)
    sh, sl = split2(s_ref[...])
    q, k, v = q_ref[...], k_ref[...], v_ref[...]
    far = mm(
        jnp.concatenate([dh, dl, dh], axis=1), jnp.concatenate([sh, sh, sl], axis=1), 1, 1
    )
    blocks, half = lower_rows(dh, v)
    qg_ref[...] = (lower_times(blocks, half, k) + far).astype(BF16)
    blocks, half = upper_rows(v, dh)
    kp_ref[...] = upper_times(blocks, half, q)
    blocks, half = upper_rows(k, q)
    vp_ref[...] = upper_times(blocks, half, dh)


def final_kernel(c_ref, kp_ref, vp_ref, k_ref, v_ref, s_ref, *refs):
    kg_ref, vg_ref = refs[-2:]
    s = s_ref[...]
    k, v = k_ref[...], v_ref[...]
    far = mm(jnp.concatenate([v, v], axis=1), split_cat(s, 1), 1, 1)
    kg_ref[...] = (kp_ref[...] + far).astype(BF16)
    far = mm(jnp.concatenate([k, k], axis=1), split_cat(s, 0), 1, 0)
    vg_ref[...] = (vp_ref[...] + far).astype(BF16)


def place_kernel(c_ref, t_ref, *refs, hg):
    s_ref, g_ref = refs[-2:]
    size = s_ref.shape[1]
    for h in range(hg):
        s_ref[h] = t_ref[h * size : (h + 1) * size, :]
    g_ref[0] = t_ref[hg * size : hg * size + hg, :]


def pick(parts, me):
    n = len(parts)
    if n == 1:
        return parts
    half = n // 2
    near, far = pick(parts[:half], me % half), pick(parts[half:], me % half)
    swap = me >= half
    return [jnp.where(swap, b, a) for a, b in zip(near, far)] + [
        jnp.where(swap, a, b) for a, b in zip(near, far)
    ]


def permute(x, n, k):
    return lax.ppermute(x, "seq", [(i, i ^ k) for i in range(n)])


def ahead(parts, me, k, reverse):
    total = None
    for j, part in enumerate(parts):
        take = ((me ^ j) > (me ^ k)) if reverse else ((me ^ j) < (me ^ k))
        if j == k:
            continue
        term = part * take.astype(F32)
        total = term if total is None else total + term
    return total


def exchange(pieces, n, me, reverse, with_total):
    c, z, planes = me % PLANE, me // PLANE, n // PLANE
    got = [pieces[0]] + [permute(pieces[k], n, k) for k in range(1, PLANE)]
    plane = got[0] + got[1] + got[2] + got[3]
    rows = plane.shape[0] // planes
    cut = [
        lax.dynamic_slice(plane, ((z ^ k) * rows, 0), (rows, plane.shape[1]))
        for k in range(planes)
    ]
    cut = cut[:1] + [permute(cut[k], n, k * PLANE) for k in range(1, planes)]
    sums = [ahead(cut, z, k, reverse) for k in range(planes)]
    back = sums[:1] + [permute(sums[k], n, k * PLANE) for k in range(1, planes)]
    outer = jnp.concatenate(pick(back, z), axis=0)
    sums = [outer + ahead(got, c, k, reverse) for k in range(PLANE)]
    found = sums[:1] + [permute(sums[k], n, k) for k in range(1, PLANE)]
    if not with_total:
        return found
    whole = sum(cut[1:], cut[0])
    back = [whole] + [permute(whole, n, k * PLANE) for k in range(1, planes)]
    outer = jnp.concatenate(pick(back, z), axis=0)
    return found, [outer] + [permute(outer, n, k) for k in range(1, PLANE)]


def per_device(query_in, key_in, value_in, upstream, norm_gain, state_in, *, n):
    heads, size = state_in.shape[:2]
    rows, width = query_in.shape
    hg = heads // PLANE
    columns = width * lax.axis_size("head")
    me = lax.axis_index("seq")
    c = (me % PLANE).astype(jnp.int32)
    c_arr = c.reshape(1)
    gain = norm_gain.reshape(1, width)
    pad = -(-(hg * size + hg) // (8 * (n // PLANE))) * (8 * (n // PLANE))
    sds = jax.ShapeDtypeStruct

    def natural(g0):
        return lambda j, cr: (0, ((g0 + j // hg) ^ cr[0]) * hg + j % hg)

    def own_order(g0):
        return lambda j, cr: (0, g0 * hg + j)

    def fixed(*shape):
        return pl.BlockSpec(shape, lambda j, cr: (0,) * len(shape))

    def tok(g0):
        return pl.BlockSpec((rows, size), natural(g0))

    def xtok(g0):
        return pl.BlockSpec((rows, size), own_order(g0))

    def gains(g0):
        return pl.BlockSpec((1, size), natural(g0))

    def call(kernel, steps, ins, in_specs, out_shapes, out_specs, name, flops, scratch=(), aliases=None):
        nbytes = sum(x.size * x.dtype.itemsize for x in out_shapes) + 4 * 2**20
        return pl.pallas_call(
            kernel,
            out_shape=out_shapes,
            grid_spec=pltpu.PrefetchScalarGridSpec(
                num_scalar_prefetch=1,
                grid=(steps,),
                in_specs=in_specs,
                out_specs=out_specs,
                scratch_shapes=list(scratch),
            ),
            input_output_aliases=aliases or {},
            compiler_params=pltpu.CompilerParams(
                dimension_semantics=("arbitrary",), vmem_limit_bytes=24 * 2**20
            ),
            cost_estimate=pl.CostEstimate(flops=flops, bytes_accessed=nbytes, transcendentals=0),
            name=name,
        )(c_arr, *ins)

    unit = 2 * rows * size * size

    def local(g0, g1):
        count = g1 - g0
        return call(
            functools.partial(local_kernel, hg=hg),
            count * hg,
            (key_in, value_in),
            [tok(g0), tok(g0)],
            [sds((hg * size, size), F32)] * count,
            [fixed(hg * size, size)] * count,
            f"local{g0}",
            unit * count * hg,
        )

    sent = local(1, PLANE)
    kept = local(0, 1)
    inside = call(
        inside_kernel,
        heads,
        (query_in, key_in, value_in),
        [tok(0)] * 3,
        [sds((rows, width), F32)],
        [xtok(0)],
        "inside",
        unit * 6 * heads,
    )[0]
    earlier = exchange(list(kept) + list(sent), n, me, False, False)

    a, state, stat = inside, None, None
    for k in range(PLANE):
        first, last = k == 0, k == PLANE - 1
        ins = [a, query_in, upstream, gain, state_in, earlier[k]]
        specs = [
            xtok(k),
            tok(k),
            tok(k),
            gains(k),
            pl.BlockSpec((1, size, size), lambda j, cr, k=k: ((k ^ cr[0]) * hg + j, 0, 0)),
            pl.BlockSpec((size, size), lambda j, cr: (j, 0)),
        ]
        aliases = {1: 0}
        if not first:
            ins += [state, stat]
            specs += [pl.BlockSpec(memory_space=pl.ANY), fixed(2, rows, size)]
            aliases[7] = 1
        shapes = [sds((rows, width), F32), sds((heads * size, size), F32), sds((2, rows, size), F32)]
        out_specs = [
            xtok(k),
            pl.BlockSpec((size, size), lambda j, cr, k=k: (k * hg + j, 0)),
            fixed(2, rows, size),
        ]
        if last:
            shapes.append(sds((2, rows), F32))
            out_specs.append(fixed(2, rows))
        out = call(
            functools.partial(carried_kernel, hg=hg, first=first, last=last),
            hg, ins, specs, shapes, out_specs, f"carried{k}", 2 * unit * hg, aliases=aliases,
        )
        a, state, stat = out[:3]
    stats = lax.psum(out[3], "head")

    terms = [pltpu.VMEM((rows, 128), F32)] * 2

    def inner(g0, g1):
        count = g1 - g0
        return call(
            functools.partial(inner_kernel, hg=hg, columns=columns),
            count * hg,
            (a, query_in, upstream, gain, stats),
            [xtok(g0), tok(g0), tok(g0), gains(g0), fixed(2, rows)],
            [sds((pad, size), F32)] * count,
            [fixed(pad, size)] * count,
            f"inner{g0}",
            unit * count * hg,
            scratch=terms,
        )

    sent = inner(1, PLANE)
    kept = inner(0, 1)
    later, totals = exchange(list(kept) + list(sent), n, me, True, True)

    parts, normed, query_grad = [], None, None
    flat = sds((rows, width), BF16)
    for k in range(PLANE):
        first = k == 0
        ins = [a, query_in, key_in, value_in, upstream, gain, stats, state]
        specs = [
            xtok(k), tok(k), tok(k), tok(k), tok(k), gains(k), fixed(2, rows),
            pl.BlockSpec((size, size), lambda j, cr, k=k: (k * hg + j, 0)),
        ]
        aliases = {}
        if not first:
            ins += [normed, query_grad]
            specs += [pl.BlockSpec(memory_space=pl.ANY)] * 2
            aliases = {9: 0, 10: 1}
        part = pl.BlockSpec((rows, size), lambda j, cr: (0, j))
        normed, query_grad, kp, vp = call(
            functools.partial(window_kernel, columns=columns, first=first),
            hg, ins, specs,
            [flat, flat] + [sds((rows, hg * size), F32)] * 2,
            [tok(k), tok(k), part, part],
            f"window{k}", 20 * unit * hg, scratch=terms, aliases=aliases,
        )
        parts.append((kp, vp))

    key_grad, value_grad = None, None
    for k in range(PLANE):
        ins = [*parts[k], key_in, value_in, later[k]]
        part = pl.BlockSpec((rows, size), lambda j, cr: (0, j))
        specs = [part, part, tok(k), tok(k), pl.BlockSpec((size, size), lambda j, cr: (j, 0))]
        aliases = {}
        if k:
            ins += [key_grad, value_grad]
            specs += [pl.BlockSpec(memory_space=pl.ANY)] * 2
            aliases = {6: 0, 7: 1}
        key_grad, value_grad = call(
            final_kernel, hg, ins, specs, [flat, flat], [tok(k), tok(k)],
            f"final{k}", 4 * unit * hg, aliases=aliases,
        )

    state_grad, gain_grad = None, None
    for k in range(PLANE):
        ins, specs, aliases = [totals[k]], [fixed(pad, size)], {}
        if k:
            ins += [state_grad, gain_grad]
            specs += [pl.BlockSpec(memory_space=pl.ANY)] * 2
            aliases = {2: 0, 3: 1}
        state_grad, gain_grad = call(
            functools.partial(place_kernel, hg=hg), 1, ins, specs,
            [sds((heads, size, size), F32), sds((PLANE, hg, size), F32)],
            [
                pl.BlockSpec((hg, size, size), lambda j, cr, k=k: (k ^ cr[0], 0, 0)),
                pl.BlockSpec((1, hg, size), lambda j, cr, k=k: (k ^ cr[0], 0, 0)),
            ],
            f"place{k}", 1, aliases=aliases,
        )
    return normed, query_grad, key_grad, value_grad, gain_grad.reshape(width), state_grad


def solution(mesh):
    rows = P("seq", "head")
    placed = (rows, rows, rows, rows, P("head"), P("head", None, None))
    return jax.shard_map(
        functools.partial(per_device, n=mesh.shape["seq"]),
        mesh=mesh,
        in_specs=placed,
        out_specs=placed,
        check_vma=False,
    )
```
